128 devices in a mesh: expert: 8 (over z, core), task: 4 (over y), shard: 4 (over x).
Axes of the slice: x: 4, y: 4, z: 4, core: 2. Of those that a mesh axis runs over, the one named last changes fastest.
Arguments:
- weights: bfloat16 [4, 8, 8192, 2048], P('task', None, ('expert', 'shard')), may hold values from -6 to 6
- fisher: bfloat16 [4, 8, 8192, 2048], P('task', None, ('expert', 'shard')), may hold values from 0.049804688 to 5
- base_weights: bfloat16 [8, 8192, 2048], P('expert', 'task', 'shard'), may hold values from -6 to 6
- tile_list: int32 [4, 8, 32, 1], P('task'), may hold values from 0 to 1, as said below
- tile_count: int32 [4, 8, 32], P('task'), may hold values from 0 to 1, as said below
Outputs:
- merged: bfloat16 [8, 8192, 2048], P('expert', 'task', 'shard')
The draws below stay inside these ranges and needn't reach their ends.
Inputs may be any that keep to these rules, and one draw needn't show every extreme that they name: `tile_list`: for each fine-fit, expert and row block the first tile_count entries are distinct tiles of the block, numbered 0 to 1, in ascending order; the remaining entries are 0. `tile_count`: 1 is reached, and for each fine-fit some expert has 1 in every row block.
All inputs are finite; a program needn't handle non-finite values.
Results may differ from the reference program's by a relative error of at most 0.006.
Values may be sent and summed in bfloat16 or wider, within the bound.
No kernel may reach another device: no remote copies, remote signals or barrier semaphores. Data moves between devices by JAX's collectives and lax.ppermute only.
A program may use at most 128 MiB of HBM per device.

```python
import math
import jax
import jax.numpy as jnp
from jax import lax

ROWS = 8192
COLS = 2048
TILE = 128
EXPERTS = 8
TASKS = 4
BLOCKS = 32
TPB = 2
CAP = 1


def tile_plan(key):
    base_key = jax.random.fold_in(key, 7)
    key_count, key_full, key_order = jax.random.split(base_key, 3)
    counts = jax.random.randint(key_count, (TASKS, EXPERTS, BLOCKS), 0, CAP + 1)
    full_expert = jax.random.randint(key_full, (TASKS,), 0, EXPERTS)
    is_full = jnp.arange(EXPERTS)[None, :, None] == full_expert[:, None, None]
    counts = jnp.where(is_full, CAP, counts).astype(jnp.int32)
    scores = jax.random.randint(key_order, (TASKS, EXPERTS, BLOCKS, TPB), 0, 1 << 20)
    scores = scores * TPB + jnp.arange(TPB)[None, None, None, :]
    chosen = jnp.argsort(scores, axis=-1)[..., :CAP]
    slot_live = jnp.arange(CAP)[None, None, None, :] < counts[..., None]
    marked = jnp.sort(jnp.where(slot_live, chosen, TPB), axis=-1)
    listed = jnp.where(marked == TPB, 0, marked).astype(jnp.int32)
    return (listed, counts)


def draw_tile_list(key, part):
    return tile_plan(key)[0]


def draw_tile_count(key, part):
    return tile_plan(key)[1]


def shard_levels(stream_key, shape, cuts, smallest, high):
    loudness, own = 1.0, jax.random.fold_in(stream_key, 6)
    for axis_at, blocks in cuts:
        steps = jnp.exp(jax.random.uniform(jax.random.fold_in(own, axis_at), (blocks,), jnp.float32, smallest / len(cuts), high / len(cuts)))
        loudness = loudness * jnp.repeat(steps, shape[axis_at] // blocks).reshape([-1 if axis == axis_at else 1 for axis in range(len(shape))])
    return loudness


def noise(rng, shape, scale, limit, cuts=(), kind=jnp.bfloat16):
    result = jax.random.normal(rng, shape, jnp.float32) * scale
    if len(cuts) > 0:
        result = shard_levels(rng, shape, cuts, -0.22, 0.18) * result
    return jnp.clip(result, min=-limit, max=limit).astype(kind)


def setup_inputs(seed: int = 0) -> dict:
    splits = jax.random.split(jax.random.key(seed), 6)
    weights = noise(splits[0], (TASKS, EXPERTS, ROWS, COLS), 1.0, 6.0, ((0, 4), (2, 32)))
    fisher = jnp.clip(jnp.exp(math.log(5.0) - 4.609084 * jax.random.uniform(splits[1], (TASKS, EXPERTS, ROWS, COLS), jnp.float32) ** shard_levels(splits[1], (TASKS, EXPERTS, ROWS, COLS), ((0, 4), (2, 32)), -0.2, 0.2)), 0.049804688, 5.0).astype(jnp.bfloat16)
    base_weights = noise(splits[2], (EXPERTS, ROWS, COLS), 1.0, 6.0, ((0, 8), (1, 4), (2, 4)))
    tile_list = draw_tile_list(jax.random.fold_in(splits[5], 71), 0)
    tile_count = draw_tile_count(jax.random.fold_in(splits[5], 71), 0)
    return dict(weights=weights, fisher=fisher, base_weights=base_weights, tile_list=tile_list, tile_count=tile_count)


PRIOR_WEIGHT = 0.5


def reference(weights, fisher, base_weights, tile_list, tile_count):
    numerator = jnp.zeros((EXPERTS, ROWS, COLS), jnp.float32)
    denominator = jnp.zeros((EXPERTS, ROWS, COLS), jnp.float32)
    for task_index in range(TASKS):
        slot_live = jnp.arange(CAP, dtype=jnp.int32)[None, None, :] < tile_count[task_index][:, :, None]
        matches = (tile_list[task_index][:, :, :, None] == jnp.arange(TPB, dtype=jnp.int32)[None, None, None, :]) & slot_live[:, :, :, None]
        kept_tiles = jnp.any(matches, axis=2).reshape(EXPERTS, BLOCKS * TPB).astype(jnp.float32)
        row_mask = jnp.repeat(kept_tiles, TILE, axis=1)[:, :, None]
        fisher_now = fisher[task_index].astype(jnp.float32) * row_mask
        term = (fisher_now * weights[task_index].astype(jnp.float32)).astype(jnp.bfloat16)
        term = lax.optimization_barrier(term)
        share = fisher_now.astype(jnp.bfloat16)
        share = lax.optimization_barrier(share)
        numerator = numerator + term.astype(jnp.float32)
        denominator = denominator + share.astype(jnp.float32)
    merged = (numerator + PRIOR_WEIGHT * base_weights.astype(jnp.float32)) / (denominator + PRIOR_WEIGHT)
    return merged.astype(jnp.bfloat16)
```

```python
import functools

import jax
import jax.numpy as jnp
from jax import lax
from jax.experimental import pallas as pl
from jax.experimental.pallas import tpu as pltpu
from jax.sharding import Mesh, PartitionSpec as P

TILE = 128
PRIOR_WEIGHT = 0.5
CHUNKS = (32, 32, 32, 32)
ANY = pl.BlockSpec(memory_space=pl.ANY)
SMEM = pl.BlockSpec(memory_space=pltpu.SMEM)


def run_all(copies):
    for c in copies:
        c.start()
    for c in copies:
        c.wait()


def pack_body(start, rows, blocks, code, weights, fisher, *rest):
    outs, sem = rest[:-1], rest[-1]
    n = len(outs)
    z = lax.axis_index("z")
    block = (z * 2 + lax.axis_index("core")) * lax.axis_size("shard") + lax.axis_index("shard")
    copies = []
    for d, out in enumerate(outs):
        for ec in range(2):
            e = lax.rem(z + d, n) * 2 + ec
            tile = jnp.maximum(code[e * blocks + block] - 1, 0)
            at = pl.ds(pl.multiple_of(tile * TILE + start, 16), rows)
            for a, src in enumerate((weights, fisher)):
                copies.append(
                    pltpu.make_async_copy(src.at[e, at], out.at[ec, a], sem.at[len(copies)])
                )
    run_all(copies)


def pack(code, weights, fisher, start, rows, n):
    blocks = code.shape[0] // weights.shape[0]
    cols = weights.shape[2]
    out = jax.ShapeDtypeStruct((2, 2, rows, cols), weights.dtype)
    return pl.pallas_call(
        functools.partial(pack_body, start, rows, blocks),
        out_shape=[out] * n,
        in_specs=[SMEM, ANY, ANY],
        out_specs=[ANY] * n,
        scratch_shapes=[pltpu.SemaphoreType.DMA((4 * n,))],
        name="pack",
    )(code, weights, fisher)


def order_body(*refs):
    n = len(refs) - 2
    out, sem = refs[n], refs[n + 1]
    z = lax.axis_index("z")
    copies = []
    for d in range(n):
        came = lax.rem(z + n - d, n)
        for ec in range(2):
            copies.append(
                pltpu.make_async_copy(refs[d].at[ec], out.at[ec * n + came], sem.at[len(copies)])
            )
    run_all(copies)


def order(pieces):
    n = len(pieces)
    p = pieces[0]
    return pl.pallas_call(
        order_body,
        out_shape=jax.ShapeDtypeStruct((2 * n, *p.shape[1:]), p.dtype),
        in_specs=[ANY] * n,
        out_specs=ANY,
        scratch_shapes=[pltpu.SemaphoreType.DMA((2 * n,))],
        name="order",
    )(*pieces)


def merge_body(blocks, code, got, base, *outs):
    n = len(outs)
    experts = code.shape[0] // (blocks * got.shape[1])
    tasks = got.shape[1]
    rows, cols = outs[0].shape[2:]
    x = lax.axis_index("shard")
    e = lax.axis_index("z") * 2 + lax.axis_index("core")
    block = (lax.axis_index("task") * 2 + pl.program_id(0)) * n + x
    codes = [code[(t * experts + e) * blocks + block] for t in range(tasks)]
    keep = [[jnp.where(c == j + 1, 1.0, 0.0).astype(jnp.float32) for j in range(2)] for c in codes]
    step = 16
    for d, out in enumerate(outs):
        column = lax.rem(x + d, n)
        at = pl.ds(pl.multiple_of(column * cols, cols), cols)
        for r in range(0, rows, step):
            num = [0.0, 0.0]
            den = [0.0, 0.0]
            for t in range(tasks):
                w = got[0, t, 0, pl.ds(r, step), at].astype(jnp.float32)
                f = got[0, t, 1, pl.ds(r, step), at].astype(jnp.float32)
                term = (f * w).astype(jnp.bfloat16).astype(jnp.float32)
                for j in range(2):
                    num[j] = num[j] + keep[t][j] * term
                    den[j] = den[j] + keep[t][j] * f
            for j in range(2):
                prior = base[column, 0, j, pl.ds(r, step), :].astype(jnp.float32)
                out[0, j, pl.ds(r, step), :] = (
                    (num[j] + PRIOR_WEIGHT * prior) / (den[j] + PRIOR_WEIGHT)
                ).astype(out.dtype)


def merge(code, got, base, start, blocks):
    _, tasks, _, rows, cols = got.shape
    n, _, _, _, piece = base.shape
    out = jax.ShapeDtypeStruct((2, 2, rows, piece), base.dtype)
    at = start // rows
    return pl.pallas_call(
        functools.partial(merge_body, blocks),
        out_shape=[out] * n,
        grid=(2,),
        in_specs=[
            SMEM,
            pl.BlockSpec((1, tasks, 2, rows, cols), lambda i: (i, 0, 0, 0, 0)),
            pl.BlockSpec((n, 1, 2, rows, piece), lambda i: (0, i, 0, at, 0)),
        ],
        out_specs=[pl.BlockSpec((1, 2, rows, piece), lambda i: (i, 0, 0, 0))] * n,
        name="merge",
    )(code, got, base)


def place_body(start, n, *refs):
    pieces, out, sem = refs[:n], refs[-2], refs[-1]
    rows = pieces[0].shape[2]
    x = lax.axis_index("shard")
    copies = []
    for d, piece in enumerate(pieces):
        came = lax.rem(x + n - d, n)
        for c in range(2):
            copies.append(
                pltpu.make_async_copy(
                    piece.at[c], out.at[c, came, :, pl.ds(start, rows)], sem.at[len(copies)]
                )
            )
    run_all(copies)


def place(pieces, whole, start):
    n = len(pieces)
    piece = pieces[0].shape[3]
    shape = jax.ShapeDtypeStruct((2, n, 2, TILE, piece), pieces[0].dtype)
    more = [] if whole is None else [whole]
    return pl.pallas_call(
        functools.partial(place_body, start, n),
        out_shape=shape,
        in_specs=[ANY] * (n + len(more)),
        out_specs=ANY,
        scratch_shapes=[pltpu.SemaphoreType.DMA((2 * n,))],
        input_output_aliases={n: 0} if more else {},
        name="place",
    )(*pieces, *more)


def shifted(x, axis, by):
    n = lax.axis_size(axis)
    return lax.ppermute(x, axis, [(i, (i + by) % n) for i in range(n)])


def local(weights, fisher, base_weights, tile_list, tile_count):
    weights, fisher = weights[0], fisher[0]
    nz, nx = lax.axis_size("z"), lax.axis_size("shard")
    blocks = tile_list.shape[2]
    cols = base_weights.shape[2]
    own = jnp.where(tile_count[0] > 0, tile_list[0, :, :, 0] + 1, 0).reshape(-1)
    base = jnp.swapaxes(base_weights.reshape(2, nx, 2 * TILE, cols), 0, 1)
    base = lax.all_to_all(base, "shard", 0, 0, tiled=True).reshape(nx, 2, 2, TILE, cols)
    codes = lax.all_gather(own, "task", axis=0, tiled=True)
    whole = None
    start = 0
    for rows in CHUNKS:
        packed = pack(own, weights, fisher, start, rows, nz)
        pieces = [packed[0]] + [shifted(packed[d], "z", d) for d in range(1, nz)]
        ready = order(pieces)
        got = lax.all_to_all(ready, ("core", "task"), 0, 0, tiled=True)
        got = got.reshape(2, -1, *got.shape[1:])
        merged = merge(codes, got, base, start, blocks)
        back = [merged[0]] + [shifted(merged[d], "shard", d) for d in range(1, nx)]
        whole = place(back, whole, start)
        start += rows
    return whole.reshape(base_weights.shape)


def solution(mesh):
    split = Mesh(
        mesh.devices.reshape(mesh.devices.shape[0] // 2, 2, *mesh.devices.shape[1:]),
        ("z", "core", "task", "shard"),
    )
    rows = ("z", "core")
    in_specs = (
        P("task", None, ("z", "core", "shard"), None),
        P("task", None, ("z", "core", "shard"), None),
        P(rows, "task", "shard"),
        P("task", None, None, None),
        P("task", None, None),
    )
    return jax.shard_map(
        local, mesh=split, in_specs=in_specs, out_specs=P(rows, "task", "shard"), check_vma=False
    )
```

```python
import functools

import jax
import jax.numpy as jnp
from jax import lax
from jax.experimental import pallas as pl
from jax.experimental.pallas import tpu as pltpu
from jax.sharding import Mesh, PartitionSpec as P

TILE = 128
PRIOR_WEIGHT = 0.5
LOW = 64
HINT = 400_000_000
GRANT = 16 << 20
MESH = ("z", "core", "task", "shard")
ANY = pl.BlockSpec(memory_space=pl.ANY)
HBM = pl.BlockSpec(memory_space=pltpu.HBM)
VMEM = pl.BlockSpec(memory_space=pltpu.VMEM)
SMEM = pl.BlockSpec(memory_space=pltpu.SMEM)
PARAMS = pltpu.CompilerParams(vmem_limit_bytes=GRANT)


def my_block():
    z, c, x = lax.axis_index("z"), lax.axis_index("core"), lax.axis_index("shard")
    return (z * 2 + c) * lax.axis_size("shard") + x


def copy_signed(items, held, sem):
    copies = [
        (
            pltpu.make_async_copy(src, held.at[i], sem.at[i]),
            pltpu.make_async_copy(held.at[i], dst, sem.at[i]),
            sign,
        )
        for i, (src, dst, sign) in enumerate(items)
    ]
    for read, _, _ in copies:
        read.start()
    for i, (read, write, sign) in enumerate(copies):
        read.wait()
        if sign is not None:
            held[i] = held[i] * sign
        write.start()
    for _, write, _ in copies:
        write.wait()


def listed(tiles, counts, e):
    tile = jnp.minimum(jnp.maximum(tiles[e, my_block()], 0), 1)
    sign = jnp.where(counts[e, my_block()] > 0, jnp.where(tile == 0, 1.0, -1.0), 0.0)
    return tile * TILE, sign.astype(jnp.bfloat16)


def pack_low_body(tiles, counts, weights, fisher, out, token, held, sem):
    token[0] = 0
    n, _, _, rows, _ = out.shape
    y = lax.axis_index("task")
    items = []
    for j in range(n):
        for ec in range(2):
            e = lax.rem(y + j, n) * 2 + ec
            row, sign = listed(tiles, counts, e)
            at = pl.ds(pl.multiple_of(row, TILE), rows)
            items.append((weights.at[e, at], out.at[j, ec, 0], None))
            items.append((fisher.at[e, at], out.at[j, ec, 1], sign))
    copy_signed(items, held, sem)


def pack_low(tiles, counts, weights, fisher, n):
    cols = weights.shape[2]
    return pl.pallas_call(
        pack_low_body,
        out_shape=[
            jax.ShapeDtypeStruct((n, 2, 2, LOW, cols), weights.dtype),
            jax.ShapeDtypeStruct((1,), jnp.int32),
        ],
        in_specs=[SMEM, SMEM, HBM, HBM],
        out_specs=[HBM, SMEM],
        scratch_shapes=[
            pltpu.VMEM((4 * n, LOW, cols), weights.dtype),
            pltpu.SemaphoreType.DMA((4 * n,)),
        ],
        name="pack_low",
    )(tiles, counts, weights, fisher)


def pack_high_body(tiles, counts, weights, fisher, after, *rest):
    outs, held, sem = rest[:-2], rest[-2], rest[-1]
    n = len(outs)
    experts, _, rows, _ = outs[0].shape
    y = lax.axis_index("task")
    items = []
    for d in (*range(1, n), 0):
        part = LOW + lax.rem(y + d, n) * rows
        for e in range(experts):
            row, sign = listed(tiles, counts, e)
            at = pl.ds(pl.multiple_of(row + part, 8), rows)
            items.append((weights.at[e, at], outs[d].at[e, 0], None))
            items.append((fisher.at[e, at], outs[d].at[e, 1], sign))
    copy_signed(items, held, sem)


def pack_high(tiles, counts, weights, fisher, n, after):
    experts, _, cols = weights.shape
    rows = (TILE - LOW) // n
    count = 2 * n * experts
    return pl.pallas_call(
        pack_high_body,
        out_shape=[jax.ShapeDtypeStruct((experts, 2, rows, cols), weights.dtype)] * n,
        in_specs=[SMEM, SMEM, HBM, HBM, SMEM],
        out_specs=[HBM] * n,
        scratch_shapes=[
            pltpu.VMEM((count, rows, cols), weights.dtype),
            pltpu.SemaphoreType.DMA((count,)),
        ],
        name="pack_high",
    )(tiles, counts, weights, fisher, after)


def sums(loads):
    num, den = [0.0, 0.0], [0.0, 0.0]
    for load in loads:
        w, f = (v.astype(jnp.float32) for v in load())
        term = (f * w).astype(jnp.bfloat16).astype(jnp.float32)
        term_0, share_0 = jnp.where(f > 0.0, term, 0.0), jnp.maximum(f, 0.0)
        num = [num[0] + term_0, num[1] + (term_0 - term)]
        den = [den[0] + share_0, den[1] + (share_0 - f)]
    return num, den


def merged_of(num, den, prior):
    return (num + PRIOR_WEIGHT * prior.astype(jnp.float32)) / (den + PRIOR_WEIGHT)


def merge_low_body(n, first, *rest):
    got, base, outs = (first, *rest[: n - 1]), rest[n - 1 : 2 * n - 1], rest[2 * n - 1 :]
    rows, cols = outs[0].shape[2:]
    x = lax.axis_index("shard")
    step = 16
    for d, out in enumerate(outs):
        at = pl.ds(pl.multiple_of(lax.rem(x + d, n) * cols, cols), cols)
        for r in range(0, rows, step):
            loads = [
                lambda g=g: (g[0, 0, pl.ds(r, step), at], g[0, 1, pl.ds(r, step), at]) for g in got
            ]
            num, den = sums(loads)
            for j in range(2):
                prior = base[(n - d) % n][0, j, pl.ds(r, step), :]
                out[0, j, pl.ds(r, step), :] = merged_of(num[j], den[j], prior).astype(out.dtype)


def merge_low(first, others, base):
    n = len(base)
    _, _, _, rows, cols = first.shape
    piece = base[0].shape[3]
    out = jax.ShapeDtypeStruct((2, 2, rows, piece), first.dtype)
    return pl.pallas_call(
        functools.partial(merge_low_body, n),
        out_shape=[out] * n,
        grid=(2,),
        in_specs=[pl.BlockSpec((None, 1, 2, rows, cols), lambda i: (0, i, 0, 0, 0))]
        + [pl.BlockSpec((1, 2, rows, cols), lambda i: (i, 0, 0, 0))] * (n - 1)
        + [pl.BlockSpec((1, 2, rows, piece), lambda i: (i, 0, 0, 0))] * n,
        out_specs=[pl.BlockSpec((1, 2, rows, piece), lambda i: (i, 0, 0, 0))] * n,
        compiler_params=PARAMS,
        cost_estimate=pl.CostEstimate(flops=0, bytes_accessed=HINT, transcendentals=0),
        name="merge_low",
    )(first, *others, *base)


def add_high_body(n, y, *refs):
    got, out = refs[:n], refs[n]
    cols = out.shape[-1]
    for x in range(n):
        at = pl.ds(x * cols, cols)
        num, den = sums([lambda g=g: (g[0, 0, :, at], g[0, 1, :, at]) for g in got])
        for j in range(2):
            out[0, x, j, 0] = num[j].astype(out.dtype)
            out[0, x, j, 1] = den[j].astype(out.dtype)


def add_high(y, got):
    n = len(got)
    experts, _, rows, cols = got[0].shape
    expert = lambda i, y: (lax.rem(y[0] + i // 2, n) * 2 + lax.rem(i, 2), 0, 0, 0)
    return pl.pallas_call(
        functools.partial(add_high_body, n),
        out_shape=jax.ShapeDtypeStruct((experts, n, 2, 2, rows, cols // n), got[0].dtype),
        grid_spec=pltpu.PrefetchScalarGridSpec(
            num_scalar_prefetch=1,
            grid=(experts,),
            in_specs=[pl.BlockSpec((1, 2, rows, cols), expert)] * n,
            out_specs=pl.BlockSpec((1, n, 2, 2, rows, cols // n), lambda i, y: (i, 0, 0, 0, 0, 0)),
        ),
        compiler_params=PARAMS,
        name="add_high",
    )(y, *got)


def place_body(n, *refs):
    pieces, out, sem = refs[:n], refs[-2], refs[-1]
    x = lax.axis_index("shard")
    copies = []
    for d, piece in enumerate(pieces):
        came = lax.rem(x + n - d, n)
        for c in range(2):
            copies.append(
                pltpu.make_async_copy(
                    piece.at[c], out.at[c, came, :, pl.ds(0, piece.shape[2])], sem.at[len(copies)]
                )
            )
    for c in copies:
        c.start()
    for c in copies:
        c.wait()


def place(pieces):
    n = len(pieces)
    return pl.pallas_call(
        functools.partial(place_body, n),
        out_shape=jax.ShapeDtypeStruct((2, n, 2, TILE, pieces[0].shape[3]), pieces[0].dtype),
        in_specs=[VMEM] * n,
        out_specs=HBM,
        scratch_shapes=[pltpu.SemaphoreType.DMA((2 * n,))],
        compiler_params=PARAMS,
        name="place",
    )(*pieces)


def merge_high_body(n, first, *rest):
    got, base, out = (first, *rest[: n - 1]), rest[n - 1], rest[-1]
    rows = first.shape[-2]
    y = lax.axis_index("task")
    for m, g in enumerate(got):
        at = pl.ds(pl.multiple_of(lax.rem(y + n - m, n) * rows, rows), rows)
        for x in range(n):
            for j in range(2):
                num, den = (g[0, x, j, k].astype(jnp.float32) for k in range(2))
                out[0, x, j, at, :] = merged_of(num, den, base[0, x, j, at, :]).astype(out.dtype)


def merge_high(first, others, base, whole):
    n = len(others) + 1
    _, c, _, _, _, rows, cols = first.shape
    block = (1, n, 2, 2, rows, cols)
    part = pl.BlockSpec((1, n, 2, TILE - LOW, cols), lambda i: (i, 0, 0, LOW // (TILE - LOW), 0))
    return pl.pallas_call(
        functools.partial(merge_high_body, n),
        out_shape=jax.ShapeDtypeStruct(whole.shape, whole.dtype),
        grid=(c,),
        in_specs=[pl.BlockSpec((None, *block), lambda i: (0, i, 0, 0, 0, 0, 0))]
        + [pl.BlockSpec(block, lambda i: (i, 0, 0, 0, 0, 0))] * (n - 1)
        + [part, HBM],
        out_specs=part,
        input_output_aliases={n + 1: 0},
        compiler_params=PARAMS,
        name="merge_high",
    )(first, *others, base, whole)


def shifted(x, axis, by):
    n = lax.axis_size(axis)
    return lax.ppermute(x, axis, [(i, (i + by) % n) for i in range(n)])


def spread(x, over_x):
    nz, ny, nx = (lax.axis_size(a) for a in ("z", "task", "shard"))
    number = lambda z, c, y, x: ((z * 2 + c) * ny + y) * nx + x
    groups = []
    for y in range(ny):
        turned = [((j + y) % nz, c) for j in range(nz) for c in range(2)]
        if over_x:
            groups.append([number(z, c, y, x) for z, c in turned for x in range(nx)])
        else:
            groups += [[number(z, c, y, x) for z, c in turned] for x in range(nx)]
    return lax.all_to_all(x, MESH, 0, 0, axis_index_groups=groups, tiled=True)


def local(weights, fisher, base_weights, tile_list, tile_count):
    weights, fisher = weights[0], fisher[0]
    nz, nx, ny = (lax.axis_size(a) for a in ("z", "shard", "task"))
    x, y = lax.axis_index("shard"), lax.axis_index("task").reshape(1)
    cols = base_weights.shape[2]
    hold = lax.optimization_barrier

    tiles, counts = tile_list[0, :, :, 0], tile_count[0]
    low, packed = pack_low(tiles, counts, weights, fisher, nz)
    high = pack_high(tiles, counts, weights, fisher, ny, packed)

    got_low = spread(low.reshape(2 * nz, *low.shape[2:]), False).reshape(low.shape)
    got_high = [high[0]] + [shifted(high[d], "task", d) for d in range(1, ny)]
    mine = [got_low[m] for m in range(1, ny)]
    mine, got_high, base = hold((mine, got_high, base_weights))
    others = [shifted(mine[m - 1], "task", m) for m in range(1, ny)]
    added = add_high(y, got_high)
    moved = spread(added.reshape(-1, *added.shape[2:]), True)
    moved = moved.reshape(nz, 2, nx, *moved.shape[1:])
    mine = [moved[m] for m in range(1, ny)]

    base = base.reshape(2, nx, 2, TILE, cols)
    prior = []
    for d in range(nx):
        part = lax.dynamic_index_in_dim(base[:, :, :, :LOW], lax.rem(x + d, nx), 1, keepdims=False)
        prior.append(shifted(part, "shard", d) if d else part)
    mine, others, prior = hold((mine, others, prior))
    rest = [shifted(mine[m - 1], "task", m) for m in range(1, ny)]

    merged = merge_low(got_low, others, prior)
    whole = place([merged[0]] + [shifted(merged[d], "shard", d) for d in range(1, nx)])
    whole = merge_high(moved, rest, base_weights.reshape(whole.shape), whole)
    return whole.reshape(base_weights.shape)


def solution(mesh):
    split = Mesh(
        mesh.devices.reshape(mesh.devices.shape[0] // 2, 2, *mesh.devices.shape[1:]), MESH
    )
    rows = ("z", "core")
    in_specs = (
        P("task", None, ("z", "core", "shard"), None),
        P("task", None, ("z", "core", "shard"), None),
        P(rows, "task", "shard"),
        P("task", None, None, None),
        P("task", None, None),
    )
    return jax.shard_map(
        local, mesh=split, in_specs=in_specs, out_specs=P(rows, "task", "shard"), check_vma=False
    )
```

```python
import functools

import jax
import jax.numpy as jnp
from jax import lax
from jax.experimental import pallas as pl
from jax.experimental.pallas import tpu as pltpu
from jax.sharding import Mesh, PartitionSpec as P

TILE = 128
PRIOR_WEIGHT = 0.5
LOW = 64
LONG = pl.CostEstimate(flops=100_000_000_000, bytes_accessed=0, transcendentals=0)
SHORT = pl.CostEstimate(flops=0, bytes_accessed=0, transcendentals=0)
GRANT = 16 << 20
MESH = ("z", "core", "task", "shard")
ANY = pl.BlockSpec(memory_space=pl.ANY)
HBM = pl.BlockSpec(memory_space=pltpu.HBM)
VMEM = pl.BlockSpec(memory_space=pltpu.VMEM)
SMEM = pl.BlockSpec(memory_space=pltpu.SMEM)
PARAMS = pltpu.CompilerParams(vmem_limit_bytes=GRANT)


def my_block():
    z, c, x = lax.axis_index("z"), lax.axis_index("core"), lax.axis_index("shard")
    return (z * 2 + c) * lax.axis_size("shard") + x


def listed(tiles, counts, e):
    tile = jnp.minimum(jnp.maximum(tiles[e, my_block()], 0), 1)
    sign = jnp.where(counts[e, my_block()] > 0, jnp.where(tile == 0, 1.0, -1.0), 0.0)
    return tile * TILE, sign.astype(jnp.bfloat16)


def pack_body(tiles, counts, weights, fisher, low, *rest):
    high, (held, came, sent) = rest[:-3], rest[-3:]
    n, rows = len(high), high[0].shape[2]
    y = lax.axis_index("task")
    reads, signs, experts = [], [], []
    for j in range(n):
        for ec in range(2):
            e = lax.rem(y + j, n) * 2 + ec
            row, sign = listed(tiles, counts, e)
            at = pl.ds(pl.multiple_of(row, TILE), TILE)
            for a, src in enumerate((weights, fisher)):
                i = len(reads)
                reads.append(pltpu.make_async_copy(src.at[e, at], held.at[i], came.at[i]))
                signs.append(sign if a else None)
                experts.append(e)
    for read in reads:
        read.start()
    writes = []
    for i, read in enumerate(reads):
        read.wait()
        if signs[i] is not None:
            held[i] = held[i] * signs[i]
        at = low.at[i // 4, i // 2 % 2, i % 2]
        parts = [(pl.ds(0, LOW), at)]
        for d in range(n):
            row = pl.multiple_of(LOW + lax.rem(y + d, n) * rows, 8)
            parts.append((pl.ds(row, rows), high[d].at[experts[i], i % 2]))
        for src, dst in parts:
            k = len(writes)
            writes.append(pltpu.make_async_copy(held.at[i, src], dst, sent.at[k]))
            writes[-1].start()
    for write in writes:
        write.wait()


def pack(tiles, counts, weights, fisher, n):
    experts, _, cols = weights.shape
    rows = (TILE - LOW) // n
    count = 2 * experts
    return pl.pallas_call(
        pack_body,
        out_shape=[jax.ShapeDtypeStruct((n, 2, 2, LOW, cols), weights.dtype)]
        + [jax.ShapeDtypeStruct((experts, 2, rows, cols), weights.dtype)] * n,
        in_specs=[SMEM, SMEM, HBM, HBM],
        out_specs=[HBM] * (n + 1),
        scratch_shapes=[
            pltpu.VMEM((count, TILE, cols), weights.dtype),
            pltpu.SemaphoreType.DMA((count,)),
            pltpu.SemaphoreType.DMA((count * (n + 1),)),
        ],
        name="pack",
    )(tiles, counts, weights, fisher)


def sums(loads):
    num, den = [0.0, 0.0], [0.0, 0.0]
    for load in loads:
        w, f = (v.astype(jnp.float32) for v in load())
        term = (f * w).astype(jnp.bfloat16).astype(jnp.float32)
        term_0, share_0 = jnp.where(f > 0.0, term, 0.0), jnp.maximum(f, 0.0)
        num = [num[0] + term_0, num[1] + (term_0 - term)]
        den = [den[0] + share_0, den[1] + (share_0 - f)]
    return num, den


def merged_of(num, den, prior):
    return (num + PRIOR_WEIGHT * prior.astype(jnp.float32)) / (den + PRIOR_WEIGHT)


def merge_low_body(n, passed, first, *rest):
    got, base, outs = (first, *rest[: n - 1]), rest[n - 1 : 2 * n - 1], rest[2 * n - 1 :]
    rows, cols = outs[0].shape[2:]
    x = lax.axis_index("shard")
    step = 16
    for d, out in enumerate(outs):
        at = pl.ds(pl.multiple_of(lax.rem(x + d, n) * cols, cols), cols)
        for r in range(0, rows, step):
            loads = [
                lambda g=g: (g[0, 0, pl.ds(r, step), at], g[0, 1, pl.ds(r, step), at]) for g in got
            ]
            num, den = sums(loads)
            for j in range(2):
                prior = base[(n - d) % n][0, j, pl.ds(r, step), :]
                out[0, j, pl.ds(r, step), :] = merged_of(num[j], den[j], prior).astype(out.dtype)


def merge_low(first, others, base, passed):
    n = len(base)
    _, _, _, rows, cols = first.shape
    piece = base[0].shape[3]
    out = jax.ShapeDtypeStruct((2, 2, rows, piece), first.dtype)
    return pl.pallas_call(
        functools.partial(merge_low_body, n),
        out_shape=[out] * n,
        grid=(2,),
        in_specs=[SMEM, pl.BlockSpec((None, 1, 2, rows, cols), lambda i: (0, i, 0, 0, 0))]
        + [pl.BlockSpec((1, 2, rows, cols), lambda i: (i, 0, 0, 0))] * (n - 1)
        + [pl.BlockSpec((1, 2, rows, piece), lambda i: (i, 0, 0, 0))] * n,
        out_specs=[pl.BlockSpec((1, 2, rows, piece), lambda i: (i, 0, 0, 0))] * n,
        compiler_params=PARAMS,
        cost_estimate=LONG,
        name="merge_low",
    )(passed, first, *others, *base)


def add_high_body(n, *refs):
    got, out = refs[:n], refs[n]
    cols = out.shape[-1]
    for e in range(out.shape[0]):
        for x in range(n):
            at = pl.ds(x * cols, cols)
            num, den = sums([lambda g=g: (g[e, 0, :, at], g[e, 1, :, at]) for g in got])
            for j in range(2):
                out[e, x, j, 0] = num[j].astype(out.dtype)
                out[e, x, j, 1] = den[j].astype(out.dtype)


def add_high(got):
    n = len(got)
    experts, _, rows, cols = got[0].shape
    step = 2
    return pl.pallas_call(
        functools.partial(add_high_body, n),
        out_shape=jax.ShapeDtypeStruct((experts, n, 2, 2, rows, cols // n), got[0].dtype),
        grid=(experts // step,),
        in_specs=[pl.BlockSpec((step, 2, rows, cols), lambda i: (i, 0, 0, 0))] * n,
        out_specs=pl.BlockSpec((step, n, 2, 2, rows, cols // n), lambda i: (i, 0, 0, 0, 0, 0)),
        compiler_params=PARAMS,
        cost_estimate=SHORT,
        name="add_high",
    )(*got)


def place_body(n, *refs):
    pieces, out, sem = refs[:n], refs[-2], refs[-1]
    x = lax.axis_index("shard")
    copies = []
    for d, piece in enumerate(pieces):
        came = lax.rem(x + n - d, n)
        for c in range(2):
            copies.append(
                pltpu.make_async_copy(
                    piece.at[c], out.at[c, came, :, pl.ds(0, piece.shape[2])], sem.at[len(copies)]
                )
            )
    for c in copies:
        c.start()
    for c in copies:
        c.wait()


def place(pieces):
    n = len(pieces)
    return pl.pallas_call(
        functools.partial(place_body, n),
        out_shape=jax.ShapeDtypeStruct((2, n, 2, TILE, pieces[0].shape[3]), pieces[0].dtype),
        in_specs=[VMEM] * n,
        out_specs=HBM,
        scratch_shapes=[pltpu.SemaphoreType.DMA((2 * n,))],
        compiler_params=PARAMS,
        cost_estimate=SHORT,
        name="place",
    )(*pieces)


def merge_high_body(got, base, *rest):
    out = rest[-1]
    n, _, _, _, _, rows, _ = got.shape
    for m in range(n):
        at = pl.ds(m * rows, rows)
        for x in range(n):
            for j in range(2):
                num, den = (got[m, 0, x, j, k].astype(jnp.float32) for k in range(2))
                out[0, x, j, at, :] = merged_of(num, den, base[0, x, j, at, :]).astype(out.dtype)


def merge_high(got, base, whole, passed):
    n, c, _, _, _, rows, cols = got.shape
    part = pl.BlockSpec((1, n, 2, TILE - LOW, cols), lambda i: (i, 0, 0, LOW // (TILE - LOW), 0))
    return pl.pallas_call(
        merge_high_body,
        out_shape=jax.ShapeDtypeStruct(whole.shape, whole.dtype),
        grid=(c,),
        in_specs=[
            pl.BlockSpec((n, 1, n, 2, 2, rows, cols), lambda i: (0, i, 0, 0, 0, 0, 0)),
            part,
            HBM,
            SMEM,
        ],
        out_specs=part,
        input_output_aliases={2: 0},
        compiler_params=PARAMS,
        name="merge_high",
    )(got, base, whole, passed)


def fence_body(*refs):
    refs[-1][0] = 0


def fence(arrays):
    return pl.pallas_call(
        fence_body,
        out_shape=jax.ShapeDtypeStruct((1,), jnp.int32),
        in_specs=[ANY] * len(arrays),
        out_specs=SMEM,
        compiler_params=PARAMS,
        cost_estimate=LONG,
        name="fence",
    )(*arrays)


def shifted(x, axis, by):
    n = lax.axis_size(axis)
    return lax.ppermute(x, axis, [(i, (i + by) % n) for i in range(n)])


def all_shifted(pieces, axis):
    n = lax.axis_size(axis)
    moved = {d: shifted(pieces[d], axis, d) for d in (*range(1, n, 2), *range(2, n, 2))}
    return [moved[d] for d in range(1, n)]


def over_z(x):
    nz, ny, nx = (lax.axis_size(a) for a in ("z", "task", "shard"))
    groups = [
        [(((j + y) % nz * 2 + c) * ny + y) * nx + x for j in range(nz) for c in range(2)]
        for y in range(ny)
        for x in range(nx)
    ]
    flat = x.reshape(2 * nz, *x.shape[2:])
    return lax.all_to_all(flat, MESH, 0, 0, axis_index_groups=groups, tiled=True).reshape(x.shape)


def local(weights, fisher, base_weights, tile_list, tile_count):
    weights, fisher = weights[0], fisher[0]
    nz, nx, ny = (lax.axis_size(a) for a in ("z", "shard", "task"))
    x = lax.axis_index("shard")
    cols = base_weights.shape[2]
    hold = lax.optimization_barrier

    tiles, counts = tile_list[0, :, :, 0], tile_count[0]
    low, *high = pack(tiles, counts, weights, fisher, nz)
    got_low = over_z(low)
    got_high = [high[0]] + all_shifted(high, "task")
    mine = [got_low[m] for m in range(1, ny)]
    base = base_weights.reshape(2, nx, 2, TILE, cols)
    base, packed = hold((base, high[1]))
    prior = []
    for d in range(nx):
        part = lax.dynamic_index_in_dim(base[:, :, :, :LOW], lax.rem(x + d, nx), 1, keepdims=False)
        prior.append(shifted(part, "shard", d) if d else part)
    mine, got_high, prior = hold((mine, got_high, prior))
    others = all_shifted([None, *mine], "task")
    added = add_high(got_high)
    moved = lax.all_to_all(
        added.reshape(-1, *added.shape[2:]), ("z", "core", "shard"), 0, 0, tiled=True
    )
    moved, passed = hold((moved, fence(others)))
    moved = lax.all_to_all(
        moved.reshape(nz, 2, nx, *moved.shape[1:]), "task", 0, 0, tiled=True
    )

    merged = merge_low(got_low, others, prior, passed)
    whole = place([merged[0]] + all_shifted(merged, "shard"))
    whole = merge_high(moved, base_weights.reshape(whole.shape), whole, passed)
    return whole.reshape(base_weights.shape)


def solution(mesh):
    split = Mesh(
        mesh.devices.reshape(mesh.devices.shape[0] // 2, 2, *mesh.devices.shape[1:]), MESH
    )
    rows = ("z", "core")
    in_specs = (
        P("task", None, ("z", "core", "shard"), None),
        P("task", None, ("z", "core", "shard"), None),
        P(rows, "task", "shard"),
        P("task", None, None, None),
        P("task", None, None),
    )
    return jax.shard_map(
        local, mesh=split, in_specs=in_specs, out_specs=P(rows, "task", "shard"), check_vma=False
    )
```

```python
import functools

import jax
import jax.numpy as jnp
from jax import lax
from jax.experimental import pallas as pl
from jax.experimental.pallas import tpu as pltpu
from jax.sharding import Mesh, PartitionSpec as P

TILE = 128
PRIOR_WEIGHT = 0.5
LOW = 64
LONG = pl.CostEstimate(flops=100_000_000_000, bytes_accessed=0, transcendentals=0)
SHORT = pl.CostEstimate(flops=0, bytes_accessed=0, transcendentals=0)
GRANT = 16 << 20
MESH = ("z", "core", "task", "shard")
ANY = pl.BlockSpec(memory_space=pl.ANY)
HBM = pl.BlockSpec(memory_space=pltpu.HBM)
VMEM = pl.BlockSpec(memory_space=pltpu.VMEM)
SMEM = pl.BlockSpec(memory_space=pltpu.SMEM)
PARAMS = pltpu.CompilerParams(vmem_limit_bytes=GRANT)


def my_block():
    z, c, x = lax.axis_index("z"), lax.axis_index("core"), lax.axis_index("shard")
    return (z * 2 + c) * lax.axis_size("shard") + x


def listed(tiles, counts, e):
    tile = jnp.minimum(jnp.maximum(tiles[e, my_block()], 0), 1)
    sign = jnp.where(counts[e, my_block()] > 0, jnp.where(tile == 0, 1.0, -1.0), 0.0)
    return tile * TILE, sign.astype(jnp.bfloat16)


def pack_body(start, rows, shifts, after, tiles, counts, weights, fisher, *refs):
    outs, (token, held, came, sent) = refs[after:-4], refs[-4:]
    token[0] = 0
    n = held.shape[0]
    y = lax.axis_index("task")
    reads = []
    for j in range(n):
        first = lax.rem(y + j, n) * 2
        for ec in range(2):
            row, sign = listed(tiles, counts, first + ec)
            if len(shifts) == 1:
                row = row + lax.rem(y + shifts[0], n) * rows
            at = pl.ds(pl.multiple_of(row + start, 8), held.shape[3])
            for a, src in enumerate((weights, fisher)):
                read = pltpu.make_async_copy(
                    src.at[first + ec, at], held.at[j, ec, a], came.at[len(reads)]
                )
                reads.append((read, sign))
                read.start()
    writes = []
    for j in range(n):
        first = lax.rem(y + j, n) * 2
        for ec in range(2):
            (read, _), (read_fisher, sign) = reads[4 * j + 2 * ec : 4 * j + 2 * ec + 2]
            read.wait()
            read_fisher.wait()
            held[j, ec, 1] = held[j, ec, 1] * sign
        parts = [(held.at[j], outs[0].at[j])] if not shifts else []
        for d, out in zip(shifts, outs):
            row = pl.multiple_of(lax.rem(y + d, n) * rows, 8) if len(shifts) > 1 else 0
            parts.append((held.at[j, :, :, pl.ds(row, rows)], out.at[pl.ds(first, 2)]))
        for src, dst in parts:
            write = pltpu.make_async_copy(src, dst, sent.at[len(writes)])
            writes.append(write)
            write.start()
    for write in writes:
        write.wait()


def pack(tiles, counts, weights, fisher, n, start, rows, shifts, after):
    experts, _, cols = weights.shape
    read = n * rows if len(shifts) > 1 else rows
    shape = (experts, 2, rows, cols) if shifts else (n, 2, 2, rows, cols)
    count = max(len(shifts), 1)
    return pl.pallas_call(
        functools.partial(pack_body, start, rows, shifts, len(after)),
        out_shape=[jax.ShapeDtypeStruct(shape, weights.dtype)] * count
        + [jax.ShapeDtypeStruct((1,), jnp.int32)],
        in_specs=[SMEM, SMEM, HBM, HBM] + [SMEM] * len(after),
        out_specs=[HBM] * count + [SMEM],
        scratch_shapes=[
            pltpu.VMEM((n, 2, 2, read, cols), weights.dtype),
            pltpu.SemaphoreType.DMA((2 * experts,)),
            pltpu.SemaphoreType.DMA((n * count,)),
        ],
        name="pack",
    )(tiles, counts, weights, fisher, *after)


def sums(loads):
    num, den = [0.0, 0.0], [0.0, 0.0]
    for load in loads:
        w, f = (v.astype(jnp.float32) for v in load())
        term = (f * w).astype(jnp.bfloat16).astype(jnp.float32)
        term_0, share_0 = jnp.where(f > 0.0, term, 0.0), jnp.maximum(f, 0.0)
        num = [num[0] + term_0, num[1] + (term_0 - term)]
        den = [den[0] + share_0, den[1] + (share_0 - f)]
    return num, den


def merged_of(num, den, prior):
    return (num + PRIOR_WEIGHT * prior.astype(jnp.float32)) / (den + PRIOR_WEIGHT)


def merge_low_body(n, passed, first, *rest):
    got, base, outs = (first, *rest[: n - 1]), rest[n - 1 : 2 * n - 1], rest[2 * n - 1 :]
    rows, cols = outs[0].shape[2:]
    x = lax.axis_index("shard")
    step = 16
    for d, out in enumerate(outs):
        at = pl.ds(pl.multiple_of(lax.rem(x + d, n) * cols, cols), cols)
        for r in range(0, rows, step):
            loads = [
                lambda g=g: (g[0, 0, pl.ds(r, step), at], g[0, 1, pl.ds(r, step), at]) for g in got
            ]
            num, den = sums(loads)
            for j in range(2):
                prior = base[(n - d) % n][0, j, pl.ds(r, step), :]
                out[0, j, pl.ds(r, step), :] = merged_of(num[j], den[j], prior).astype(out.dtype)


def merge_low(first, others, base, passed):
    n = len(base)
    _, _, _, rows, cols = first.shape
    piece = base[0].shape[3]
    out = jax.ShapeDtypeStruct((2, 2, rows, piece), first.dtype)
    return pl.pallas_call(
        functools.partial(merge_low_body, n),
        out_shape=[out] * n,
        grid=(2,),
        in_specs=[SMEM, pl.BlockSpec((None, 1, 2, rows, cols), lambda i: (0, i, 0, 0, 0))]
        + [pl.BlockSpec((1, 2, rows, cols), lambda i: (i, 0, 0, 0))] * (n - 1)
        + [pl.BlockSpec((1, 2, rows, piece), lambda i: (i, 0, 0, 0))] * n,
        out_specs=[pl.BlockSpec((1, 2, rows, piece), lambda i: (i, 0, 0, 0))] * n,
        compiler_params=PARAMS,
        cost_estimate=LONG,
        name="merge_low",
    )(passed, first, *others, *base)


def add_high_body(n, *refs):
    got, out = refs[:n], refs[n]
    cols = out.shape[-1]
    for e in range(out.shape[0]):
        for x in range(n):
            at = pl.ds(x * cols, cols)
            num, den = sums([lambda g=g: (g[e, 0, :, at], g[e, 1, :, at]) for g in got])
            for j in range(2):
                out[e, x, j, 0] = num[j].astype(out.dtype)
                out[e, x, j, 1] = den[j].astype(out.dtype)


def add_high(got):
    n = len(got)
    experts, _, rows, cols = got[0].shape
    step = 2
    return pl.pallas_call(
        functools.partial(add_high_body, n),
        out_shape=jax.ShapeDtypeStruct((experts, n, 2, 2, rows, cols // n), got[0].dtype),
        grid=(experts // step,),
        in_specs=[pl.BlockSpec((step, 2, rows, cols), lambda i: (i, 0, 0, 0))] * n,
        out_specs=pl.BlockSpec((step, n, 2, 2, rows, cols // n), lambda i: (i, 0, 0, 0, 0, 0)),
        compiler_params=PARAMS,
        cost_estimate=SHORT,
        name="add_high",
    )(*got)


def place_body(n, *refs):
    pieces, out, sem = refs[:n], refs[-2], refs[-1]
    x = lax.axis_index("shard")
    copies = []
    for d, piece in enumerate(pieces):
        came = lax.rem(x + n - d, n)
        for c in range(2):
            copies.append(
                pltpu.make_async_copy(
                    piece.at[c], out.at[c, came, :, pl.ds(0, piece.shape[2])], sem.at[len(copies)]
                )
            )
    for c in copies:
        c.start()
    for c in copies:
        c.wait()


def place(pieces):
    n = len(pieces)
    return pl.pallas_call(
        functools.partial(place_body, n),
        out_shape=jax.ShapeDtypeStruct((2, n, 2, TILE, pieces[0].shape[3]), pieces[0].dtype),
        in_specs=[VMEM] * n,
        out_specs=HBM,
        scratch_shapes=[pltpu.SemaphoreType.DMA((2 * n,))],
        compiler_params=PARAMS,
        cost_estimate=SHORT,
        name="place",
    )(*pieces)


def merge_high_body(got, base, *rest):
    out = rest[-1]
    n, _, _, _, _, rows, _ = got.shape
    for m in range(n):
        at = pl.ds(m * rows, rows)
        for x in range(n):
            for j in range(2):
                num, den = (got[m, 0, x, j, k].astype(jnp.float32) for k in range(2))
                out[0, x, j, at, :] = merged_of(num, den, base[0, x, j, at, :]).astype(out.dtype)


def merge_high(got, base, whole, passed):
    n, c, _, _, _, rows, cols = got.shape
    part = pl.BlockSpec((1, n, 2, TILE - LOW, cols), lambda i: (i, 0, 0, LOW // (TILE - LOW), 0))
    return pl.pallas_call(
        merge_high_body,
        out_shape=jax.ShapeDtypeStruct(whole.shape, whole.dtype),
        grid=(c,),
        in_specs=[
            pl.BlockSpec((n, 1, n, 2, 2, rows, cols), lambda i: (0, i, 0, 0, 0, 0, 0)),
            part,
            HBM,
            SMEM,
        ],
        out_specs=part,
        input_output_aliases={2: 0},
        name="merge_high",
    )(got, base, whole, passed)


def fence_body(*refs):
    refs[-1][0] = 0


def fence(arrays):
    return pl.pallas_call(
        fence_body,
        out_shape=jax.ShapeDtypeStruct((1,), jnp.int32),
        in_specs=[ANY] * len(arrays),
        out_specs=SMEM,
        compiler_params=PARAMS,
        cost_estimate=LONG,
        name="fence",
    )(*arrays)


def shifted(x, axis, by):
    n = lax.axis_size(axis)
    return lax.ppermute(x, axis, [(i, (i + by) % n) for i in range(n)])


def all_shifted(pieces, axis):
    n = lax.axis_size(axis)
    moved = {d: shifted(pieces[d], axis, d) for d in (*range(1, n, 2), *range(2, n, 2))}
    return [moved[d] for d in range(1, n)]


def over_z(x):
    nz, ny, nx = (lax.axis_size(a) for a in ("z", "task", "shard"))
    groups = [
        [(((j + y) % nz * 2 + c) * ny + y) * nx + x for j in range(nz) for c in range(2)]
        for y in range(ny)
        for x in range(nx)
    ]
    flat = x.reshape(2 * nz, *x.shape[2:])
    return lax.all_to_all(flat, MESH, 0, 0, axis_index_groups=groups, tiled=True).reshape(x.shape)


def local(weights, fisher, base_weights, tile_list, tile_count):
    weights, fisher = weights[0], fisher[0]
    nz, nx, ny = (lax.axis_size(a) for a in ("z", "shard", "task"))
    x = lax.axis_index("shard")
    cols = base_weights.shape[2]
    hold = lax.optimization_barrier

    tiles, counts = tile_list[0, :, :, 0], tile_count[0]
    rows = (TILE - LOW) // ny
    args = (tiles, counts, weights, fisher, nz)
    low, token = pack(*args, 0, LOW, (), ())
    high_2, token = pack(*args, LOW, rows, (2,), (token,))
    high_1, high_3, high_0, _ = pack(*args, LOW, rows, (1, 3, 0), (token,))
    high = [high_0, high_1, high_2, high_3]

    got_low = over_z(low)
    got_high = [high[0]] + all_shifted(high, "task")
    mine = [got_low[m] for m in range(1, ny)]
    base = base_weights.reshape(2, nx, 2, TILE, cols)
    base, packed = hold((base, high[1]))
    prior = []
    for d in range(nx):
        part = lax.dynamic_index_in_dim(base[:, :, :, :LOW], lax.rem(x + d, nx), 1, keepdims=False)
        prior.append(shifted(part, "shard", d) if d else part)
    mine, got_high, prior = hold((mine, got_high, prior))
    others = all_shifted([None, *mine], "task")
    added = add_high(got_high)
    moved = lax.all_to_all(
        added.reshape(-1, *added.shape[2:]), ("z", "core", "shard"), 0, 0, tiled=True
    )
    moved, passed = hold((moved, fence(others[1:2])))
    moved = lax.all_to_all(
        moved.reshape(nz, 2, nx, *moved.shape[1:]), "task", 0, 0, tiled=True
    )

    merged = merge_low(got_low, others, prior, passed)
    whole = place([merged[0]] + all_shifted(merged, "shard"))
    whole = merge_high(moved, base_weights.reshape(whole.shape), whole, passed)
    return whole.reshape(base_weights.shape)


def solution(mesh):
    split = Mesh(
        mesh.devices.reshape(mesh.devices.shape[0] // 2, 2, *mesh.devices.shape[1:]), MESH
    )
    rows = ("z", "core")
    in_specs = (
        P("task", None, ("z", "core", "shard"), None),
        P("task", None, ("z", "core", "shard"), None),
        P(rows, "task", "shard"),
        P("task", None, None, None),
        P("task", None, None),
    )
    return jax.shard_map(
        local, mesh=split, in_specs=in_specs, out_specs=P(rows, "task", "shard"), check_vma=False
    )
```

```python
import functools

import jax
import jax.numpy as jnp
from jax import lax
from jax.experimental import pallas as pl
from jax.experimental.pallas import tpu as pltpu
from jax.sharding import Mesh, PartitionSpec as P

TILE = 128
PRIOR_WEIGHT = 0.5
LOW = 64
LONG = pl.CostEstimate(flops=100_000_000_000, bytes_accessed=0, transcendentals=0)
SHORT = pl.CostEstimate(flops=0, bytes_accessed=0, transcendentals=0)
GRANT = 16 << 20
MESH = ("z", "core", "task", "shard")
ANY = pl.BlockSpec(memory_space=pl.ANY)
HBM = pl.BlockSpec(memory_space=pltpu.HBM)
VMEM = pl.BlockSpec(memory_space=pltpu.VMEM)
SMEM = pl.BlockSpec(memory_space=pltpu.SMEM)
PARAMS = pltpu.CompilerParams(vmem_limit_bytes=GRANT)


def my_block():
    z, c, x = lax.axis_index("z"), lax.axis_index("core"), lax.axis_index("shard")
    return (z * 2 + c) * lax.axis_size("shard") + x


def listed(tiles, counts, e):
    tile = jnp.minimum(jnp.maximum(tiles[e, my_block()], 0), 1)
    sign = jnp.where(counts[e, my_block()] > 0, jnp.where(tile == 0, 1.0, -1.0), 0.0)
    return tile * TILE, sign.astype(jnp.bfloat16)


def pack_body(low, rows, shifts, after, tiles, counts, weights, fisher, *refs):
    refs = refs[after:]
    count = int(low) + len(shifts)
    outs, token, helds, (came, sent) = refs[:count], refs[count], refs[count + 1 : -2], refs[-2:]
    token[0] = 0
    n = helds[0].shape[0]
    y = lax.axis_index("task")
    reads = []
    for j in range(n):
        first = lax.rem(y + j, n) * 2
        for ec in range(2):
            row, sign = listed(tiles, counts, first + ec)
            for k, held in enumerate(helds):
                at = row
                if not low or k:
                    at = at + LOW
                    if len(shifts) == 1:
                        at = at + lax.rem(y + shifts[0], n) * rows
                at = pl.ds(pl.multiple_of(at, 8), held.shape[3])
                for a, src in enumerate((weights, fisher)):
                    read = pltpu.make_async_copy(
                        src.at[first + ec, at], held.at[j, ec, a], came.at[len(reads)]
                    )
                    reads.append((read, held.at[j, ec, a], sign if a else None))
                    read.start()
    writes, per = [], len(reads) // n
    for j in range(n):
        first = lax.rem(y + j, n) * 2
        for read, held, sign in reads[j * per : (j + 1) * per]:
            read.wait()
            if sign is not None:
                held[...] = held[...] * sign
        parts = [(helds[0].at[j], outs[0].at[j])] if low else []
        for d, out in zip(shifts, outs[int(low) :]):
            row = pl.multiple_of(lax.rem(y + d, n) * rows, 8) if len(shifts) > 1 else 0
            parts.append((helds[-1].at[j, :, :, pl.ds(row, rows)], out.at[pl.ds(first, 2)]))
        for src, dst in parts:
            write = pltpu.make_async_copy(src, dst, sent.at[len(writes)])
            writes.append(write)
            write.start()
    for write in writes:
        write.wait()


def pack(tiles, counts, weights, fisher, n, low, rows, shifts, after):
    experts, _, cols = weights.shape
    reads = ([LOW] if low else []) + [n * rows if len(shifts) > 1 else rows]
    shapes = [(n, 2, 2, LOW, cols)] if low else []
    shapes += [(experts, 2, rows, cols)] * len(shifts)
    return pl.pallas_call(
        functools.partial(pack_body, low, rows, shifts, len(after)),
        out_shape=[jax.ShapeDtypeStruct(shape, weights.dtype) for shape in shapes]
        + [jax.ShapeDtypeStruct((1,), jnp.int32)],
        in_specs=[SMEM, SMEM, HBM, HBM] + [SMEM] * len(after),
        out_specs=[HBM] * len(shapes) + [SMEM],
        scratch_shapes=[pltpu.VMEM((n, 2, 2, r, cols), weights.dtype) for r in reads]
        + [
            pltpu.SemaphoreType.DMA((2 * experts * len(reads),)),
            pltpu.SemaphoreType.DMA((n * len(shapes),)),
        ],
        name="pack",
    )(tiles, counts, weights, fisher, *after)


def sums(loads):
    num, den = [0.0, 0.0], [0.0, 0.0]
    for load in loads:
        w, f = (v.astype(jnp.float32) for v in load())
        term = (f * w).astype(jnp.bfloat16).astype(jnp.float32)
        term_0, share_0 = jnp.where(f > 0.0, term, 0.0), jnp.maximum(f, 0.0)
        num = [num[0] + term_0, num[1] + (term_0 - term)]
        den = [den[0] + share_0, den[1] + (share_0 - f)]
    return num, den


def merged_of(num, den, prior):
    return (num + PRIOR_WEIGHT * prior.astype(jnp.float32)) / (den + PRIOR_WEIGHT)


def merge_low_body(n, passed, first, *rest):
    got, base, outs = (first, *rest[: n - 1]), rest[n - 1 : 2 * n - 1], rest[2 * n - 1 :]
    rows, cols = outs[0].shape[2:]
    x = lax.axis_index("shard")
    step = 16
    for d, out in enumerate(outs):
        at = pl.ds(pl.multiple_of(lax.rem(x + d, n) * cols, cols), cols)
        for r in range(0, rows, step):
            loads = [
                lambda g=g: (g[0, 0, pl.ds(r, step), at], g[0, 1, pl.ds(r, step), at]) for g in got
            ]
            num, den = sums(loads)
            for j in range(2):
                prior = base[(n - d) % n][0, j, pl.ds(r, step), :]
                out[0, j, pl.ds(r, step), :] = merged_of(num[j], den[j], prior).astype(out.dtype)


def merge_low(first, others, base, passed):
    n = len(base)
    _, _, _, rows, cols = first.shape
    piece = base[0].shape[3]
    out = jax.ShapeDtypeStruct((2, 2, rows, piece), first.dtype)
    return pl.pallas_call(
        functools.partial(merge_low_body, n),
        out_shape=[out] * n,
        grid=(2,),
        in_specs=[SMEM, pl.BlockSpec((None, 1, 2, rows, cols), lambda i: (0, i, 0, 0, 0))]
        + [pl.BlockSpec((1, 2, rows, cols), lambda i: (i, 0, 0, 0))] * (n - 1)
        + [pl.BlockSpec((1, 2, rows, piece), lambda i: (i, 0, 0, 0))] * n,
        out_specs=[pl.BlockSpec((1, 2, rows, piece), lambda i: (i, 0, 0, 0))] * n,
        compiler_params=PARAMS,
        cost_estimate=LONG,
        name="merge_low",
    )(passed, first, *others, *base)


def add_high_body(n, *refs):
    got, out = refs[:n], refs[n]
    cols = out.shape[-1]
    for e in range(out.shape[0]):
        for x in range(n):
            at = pl.ds(x * cols, cols)
            num, den = sums([lambda g=g: (g[e, 0, :, at], g[e, 1, :, at]) for g in got])
            for j in range(2):
                out[e, x, j, 0] = num[j].astype(out.dtype)
                out[e, x, j, 1] = den[j].astype(out.dtype)


def add_high(got):
    n = len(got)
    experts, _, rows, cols = got[0].shape
    step = 2
    return pl.pallas_call(
        functools.partial(add_high_body, n),
        out_shape=jax.ShapeDtypeStruct((experts, n, 2, 2, rows, cols // n), got[0].dtype),
        grid=(experts // step,),
        in_specs=[pl.BlockSpec((step, 2, rows, cols), lambda i: (i, 0, 0, 0))] * n,
        out_specs=pl.BlockSpec((step, n, 2, 2, rows, cols // n), lambda i: (i, 0, 0, 0, 0, 0)),
        compiler_params=PARAMS,
        cost_estimate=SHORT,
        name="add_high",
    )(*got)


def place_body(n, *refs):
    pieces, out, sem = refs[:n], refs[-2], refs[-1]
    x = lax.axis_index("shard")
    copies = []
    for d, piece in enumerate(pieces):
        came = lax.rem(x + n - d, n)
        for c in range(2):
            copies.append(
                pltpu.make_async_copy(
                    piece.at[c], out.at[c, came, :, pl.ds(0, piece.shape[2])], sem.at[len(copies)]
                )
            )
    for c in copies:
        c.start()
    for c in copies:
        c.wait()


def place(pieces):
    n = len(pieces)
    return pl.pallas_call(
        functools.partial(place_body, n),
        out_shape=jax.ShapeDtypeStruct((2, n, 2, TILE, pieces[0].shape[3]), pieces[0].dtype),
        in_specs=[VMEM] * n,
        out_specs=HBM,
        scratch_shapes=[pltpu.SemaphoreType.DMA((2 * n,))],
        compiler_params=PARAMS,
        cost_estimate=SHORT,
        name="place",
    )(*pieces)


def merge_high_body(got, base, *refs):
    out, held, prior, result, came, sent = refs[-6:]
    n, cores, _, _, _, rows, _ = got.shape
    high = pl.ds(LOW, TILE - LOW)
    parts = [(c, pl.ds(x, 2)) for c in range(cores) for x in range(0, n, 2)]
    reads = []
    for i, (c, x) in enumerate(parts):
        pair = [
            pltpu.make_async_copy(base.at[c, x, :, high], prior.at[i], came.at[2 * i]),
            pltpu.make_async_copy(got.at[:, c, x], held.at[i], came.at[2 * i + 1]),
        ]
        for read in pair:
            read.start()
        reads.append(pair)
    writes = []
    for i, (c, x) in enumerate(parts):
        for read in reads[i]:
            read.wait()
        for m in range(n):
            at = pl.ds(m * rows, rows)
            for k in range(2):
                for j in range(2):
                    num, den = (held[i, m, k, j, v].astype(jnp.float32) for v in range(2))
                    done = merged_of(num, den, prior[i, k, j, at, :])
                    result[i, k, j, at, :] = done.astype(out.dtype)
        writes.append(pltpu.make_async_copy(result.at[i], out.at[c, x, :, high], sent.at[i]))
        writes[-1].start()
    for write in writes:
        write.wait()


def merge_high(got, base, whole, passed):
    n, cores, _, _, _, rows, cols = got.shape
    parts = cores * n // 2
    block = (parts, 2, 2, TILE - LOW, cols)
    return pl.pallas_call(
        merge_high_body,
        out_shape=jax.ShapeDtypeStruct(whole.shape, whole.dtype),
        in_specs=[HBM, HBM, HBM, SMEM],
        out_specs=HBM,
        scratch_shapes=[
            pltpu.VMEM((parts, n, 2, 2, 2, rows, cols), got.dtype),
            pltpu.VMEM(block, base.dtype),
            pltpu.VMEM(block, whole.dtype),
            pltpu.SemaphoreType.DMA((2 * parts,)),
            pltpu.SemaphoreType.DMA((parts,)),
        ],
        input_output_aliases={2: 0},
        name="merge_high",
    )(got, base, whole, passed)


def fence_body(*refs):
    refs[-1][0] = 0


def fence(arrays):
    return pl.pallas_call(
        fence_body,
        out_shape=jax.ShapeDtypeStruct((1,), jnp.int32),
        in_specs=[ANY] * len(arrays),
        out_specs=SMEM,
        compiler_params=PARAMS,
        cost_estimate=LONG,
        name="fence",
    )(*arrays)


def shifted(x, axis, by):
    n = lax.axis_size(axis)
    return lax.ppermute(x, axis, [(i, (i + by) % n) for i in range(n)])


def all_shifted(pieces, axis):
    n = lax.axis_size(axis)
    moved = {d: shifted(pieces[d], axis, d) for d in (*range(1, n, 2), *range(2, n, 2))}
    return [moved[d] for d in range(1, n)]


def over_z(x):
    nz, ny, nx = (lax.axis_size(a) for a in ("z", "task", "shard"))
    groups = [
        [(((j + y) % nz * 2 + c) * ny + y) * nx + x for j in range(nz) for c in range(2)]
        for y in range(ny)
        for x in range(nx)
    ]
    flat = x.reshape(2 * nz, *x.shape[2:])
    return lax.all_to_all(flat, MESH, 0, 0, axis_index_groups=groups, tiled=True).reshape(x.shape)


def local(weights, fisher, base_weights, tile_list, tile_count):
    weights, fisher = weights[0], fisher[0]
    nz, nx, ny = (lax.axis_size(a) for a in ("z", "shard", "task"))
    x = lax.axis_index("shard")
    cols = base_weights.shape[2]
    hold = lax.optimization_barrier

    tiles, counts = tile_list[0, :, :, 0], tile_count[0]
    rows = (TILE - LOW) // ny
    args = (tiles, counts, weights, fisher, nz)
    low, high_2, token = pack(*args, True, rows, (2,), ())
    high_1, high_3, high_0, _ = pack(*args, False, rows, (1, 3, 0), (token,))
    high = [high_0, high_1, high_2, high_3]

    got_low = over_z(low)
    got_high = [high[0]] + all_shifted(high, "task")
    base = base_weights.reshape(2, nx, 2, TILE, cols)
    base, packed = hold((base, high[1]))
    prior = []
    for d in range(nx):
        part = lax.dynamic_index_in_dim(base[:, :, :, :LOW], lax.rem(x + d, nx), 1, keepdims=False)
        prior.append(shifted(part, "shard", d) if d else part)
    far, got_high, prior = hold((got_low[2], got_high, prior))
    far = shifted(far, "task", 2)
    added = add_high(got_high)
    near, added = hold((got_low, added))
    others = [shifted(near[1], "task", 1), far, shifted(near[3], "task", 3)]
    moved = lax.all_to_all(
        added.reshape(-1, *added.shape[2:]), ("z", "core", "shard"), 0, 0, tiled=True
    )
    moved, passed = hold((moved, fence(others[1:2])))
    moved = lax.all_to_all(
        moved.reshape(nz, 2, nx, *moved.shape[1:]), "task", 0, 0, tiled=True
    )

    merged = merge_low(got_low, others, prior, passed)
    whole = place([merged[0]] + all_shifted(merged, "shard"))
    whole = merge_high(moved, base_weights.reshape(whole.shape), whole, passed)
    return whole.reshape(base_weights.shape)


def solution(mesh):
    split = Mesh(
        mesh.devices.reshape(mesh.devices.shape[0] // 2, 2, *mesh.devices.shape[1:]), MESH
    )
    rows = ("z", "core")
    in_specs = (
        P("task", None, ("z", "core", "shard"), None),
        P("task", None, ("z", "core", "shard"), None),
        P(rows, "task", "shard"),
        P("task", None, None, None),
        P("task", None, None),
    )
    return jax.shard_map(
        local, mesh=split, in_specs=in_specs, out_specs=P(rows, "task", "shard"), check_vma=False
    )
```

```python
import functools

import jax
import jax.numpy as jnp
from jax import lax
from jax.experimental import pallas as pl
from jax.experimental.pallas import tpu as pltpu
from jax.sharding import Mesh, PartitionSpec as P

TILE = 128
PRIOR_WEIGHT = 0.5
LOW = 64
LONG = pl.CostEstimate(flops=100_000_000_000, bytes_accessed=0, transcendentals=0)
SHORT = pl.CostEstimate(flops=0, bytes_accessed=0, transcendentals=0)
GRANT = 16 << 20
MESH = ("z", "core", "task", "shard")
ANY = pl.BlockSpec(memory_space=pl.ANY)
HBM = pl.BlockSpec(memory_space=pltpu.HBM)
VMEM = pl.BlockSpec(memory_space=pltpu.VMEM)
SMEM = pl.BlockSpec(memory_space=pltpu.SMEM)
PARAMS = pltpu.CompilerParams(vmem_limit_bytes=GRANT)


def my_block():
    z, c, x = lax.axis_index("z"), lax.axis_index("core"), lax.axis_index("shard")
    return (z * 2 + c) * lax.axis_size("shard") + x


def listed(tiles, counts, e):
    tile = jnp.minimum(jnp.maximum(tiles[e, my_block()], 0), 1)
    sign = jnp.where(counts[e, my_block()] > 0, jnp.where(tile == 0, 1.0, -1.0), 0.0)
    return tile * TILE, sign.astype(jnp.bfloat16)


def pack_body(low, rows, shifts, after, tiles, counts, weights, fisher, *refs):
    refs = refs[after:]
    count = int(low) + len(shifts)
    outs, token, helds, (came, sent) = refs[:count], refs[count], refs[count + 1 : -2], refs[-2:]
    token[0] = 0
    n = helds[0].shape[0]
    y = lax.axis_index("task")
    reads = []
    for j in range(n):
        first = lax.rem(y + j, n) * 2
        for ec in range(2):
            row, sign = listed(tiles, counts, first + ec)
            for k, held in enumerate(helds):
                at = row
                if not low or k:
                    at = at + LOW
                    if len(shifts) == 1:
                        at = at + lax.rem(y + shifts[0], n) * rows
                at = pl.ds(pl.multiple_of(at, 8), held.shape[3])
                for a, src in enumerate((weights, fisher)):
                    read = pltpu.make_async_copy(
                        src.at[first + ec, at], held.at[j, ec, a], came.at[len(reads)]
                    )
                    reads.append((read, held.at[j, ec, a], sign if a else None))
                    read.start()
    writes, per = [], len(reads) // n
    for j in range(n):
        first = lax.rem(y + j, n) * 2
        for read, held, sign in reads[j * per : (j + 1) * per]:
            read.wait()
            if sign is not None:
                held[...] = held[...] * sign
        parts = [(helds[0].at[j], outs[0].at[j])] if low else []
        for d, out in zip(shifts, outs[int(low) :]):
            row = pl.multiple_of(lax.rem(y + d, n) * rows, 8) if len(shifts) > 1 else 0
            parts.append((helds[-1].at[j, :, :, pl.ds(row, rows)], out.at[pl.ds(first, 2)]))
        for src, dst in parts:
            write = pltpu.make_async_copy(src, dst, sent.at[len(writes)])
            writes.append(write)
            write.start()
    for write in writes:
        write.wait()


def pack(tiles, counts, weights, fisher, n, low, rows, shifts, after):
    experts, _, cols = weights.shape
    reads = ([LOW] if low else []) + [n * rows if len(shifts) > 1 else rows]
    shapes = [(n, 2, 2, LOW, cols)] if low else []
    shapes += [(experts, 2, rows, cols)] * len(shifts)
    return pl.pallas_call(
        functools.partial(pack_body, low, rows, shifts, len(after)),
        out_shape=[jax.ShapeDtypeStruct(shape, weights.dtype) for shape in shapes]
        + [jax.ShapeDtypeStruct((1,), jnp.int32)],
        in_specs=[SMEM, SMEM, HBM, HBM] + [SMEM] * len(after),
        out_specs=[HBM] * len(shapes) + [SMEM],
        scratch_shapes=[pltpu.VMEM((n, 2, 2, r, cols), weights.dtype) for r in reads]
        + [
            pltpu.SemaphoreType.DMA((2 * experts * len(reads),)),
            pltpu.SemaphoreType.DMA((n * len(shapes),)),
        ],
        name="pack",
    )(tiles, counts, weights, fisher, *after)


def sums(loads):
    num, den = [0.0, 0.0], [0.0, 0.0]
    for load in loads:
        w, f = (v.astype(jnp.float32) for v in load())
        term = (f * w).astype(jnp.bfloat16).astype(jnp.float32)
        term_0, share_0 = jnp.where(f > 0.0, term, 0.0), jnp.maximum(f, 0.0)
        num = [num[0] + term_0, num[1] + (term_0 - term)]
        den = [den[0] + share_0, den[1] + (share_0 - f)]
    return num, den


def merged_of(num, den, prior):
    return (num + PRIOR_WEIGHT * prior.astype(jnp.float32)) / (den + PRIOR_WEIGHT)


def merge_low_body(n, passed, first, *rest):
    got, base, outs = (first, *rest[: n - 1]), rest[n - 1 : 2 * n - 1], rest[2 * n - 1 :]
    rows, cols = outs[0].shape[2:]
    x = lax.axis_index("shard")
    step = 16
    for d, out in enumerate(outs):
        at = pl.ds(pl.multiple_of(lax.rem(x + d, n) * cols, cols), cols)
        for r in range(0, rows, step):
            loads = [
                lambda g=g: (g[0, 0, pl.ds(r, step), at], g[0, 1, pl.ds(r, step), at]) for g in got
            ]
            num, den = sums(loads)
            for j in range(2):
                prior = base[(n - d) % n][0, j, pl.ds(r, step), :]
                out[0, j, pl.ds(r, step), :] = merged_of(num[j], den[j], prior).astype(out.dtype)


def merge_low(first, others, base, passed):
    n = len(base)
    _, _, _, rows, cols = first.shape
    piece = base[0].shape[3]
    out = jax.ShapeDtypeStruct((2, 2, rows, piece), first.dtype)
    return pl.pallas_call(
        functools.partial(merge_low_body, n),
        out_shape=[out] * n,
        grid=(2,),
        in_specs=[SMEM, pl.BlockSpec((None, 1, 2, rows, cols), lambda i: (0, i, 0, 0, 0))]
        + [pl.BlockSpec((1, 2, rows, cols), lambda i: (i, 0, 0, 0))] * (n - 1)
        + [pl.BlockSpec((1, 2, rows, piece), lambda i: (i, 0, 0, 0))] * n,
        out_specs=[pl.BlockSpec((1, 2, rows, piece), lambda i: (i, 0, 0, 0))] * n,
        compiler_params=PARAMS,
        cost_estimate=LONG,
        name="merge_low",
    )(passed, first, *others, *base)


def add_high_body(n, *refs):
    got, out = refs[:n], refs[n]
    cols = out.shape[-1]
    for e in range(out.shape[0]):
        for x in range(n):
            at = pl.ds(x * cols, cols)
            num, den = sums([lambda g=g: (g[e, 0, :, at], g[e, 1, :, at]) for g in got])
            for j in range(2):
                out[e, x, j, 0] = num[j].astype(out.dtype)
                out[e, x, j, 1] = den[j].astype(out.dtype)


def add_high(got):
    n = len(got)
    experts, _, rows, cols = got[0].shape
    step = 4
    return pl.pallas_call(
        functools.partial(add_high_body, n),
        out_shape=jax.ShapeDtypeStruct((experts, n, 2, 2, rows, cols // n), got[0].dtype),
        grid=(experts // step,),
        in_specs=[pl.BlockSpec((step, 2, rows, cols), lambda i: (i, 0, 0, 0))] * n,
        out_specs=pl.BlockSpec((step, n, 2, 2, rows, cols // n), lambda i: (i, 0, 0, 0, 0, 0)),
        compiler_params=PARAMS,
        cost_estimate=SHORT,
        name="add_high",
    )(*got)


def place_body(n, *refs):
    pieces, out, sem = refs[:n], refs[-2], refs[-1]
    x = lax.axis_index("shard")
    copies = []
    for d, piece in enumerate(pieces):
        came = lax.rem(x + n - d, n)
        for c in range(2):
            copies.append(
                pltpu.make_async_copy(
                    piece.at[c], out.at[c, came, :, pl.ds(0, piece.shape[2])], sem.at[len(copies)]
                )
            )
    for c in copies:
        c.start()
    for c in copies:
        c.wait()


def place(pieces):
    n = len(pieces)
    return pl.pallas_call(
        functools.partial(place_body, n),
        out_shape=jax.ShapeDtypeStruct((2, n, 2, TILE, pieces[0].shape[3]), pieces[0].dtype),
        in_specs=[VMEM] * n,
        out_specs=HBM,
        scratch_shapes=[pltpu.SemaphoreType.DMA((2 * n,))],
        compiler_params=PARAMS,
        cost_estimate=SHORT,
        name="place",
    )(*pieces)


def merge_high_body(got, base, *refs):
    out, held, prior, result, came, sent = refs[-6:]
    n, cores, _, _, _, rows, _ = got.shape
    high = pl.ds(LOW, TILE - LOW)
    parts = [(c, pl.ds(x, 2)) for c in range(cores) for x in range(0, n, 2)]
    reads = []
    for i, (c, x) in enumerate(parts):
        pair = [
            pltpu.make_async_copy(base.at[c, x, :, high], prior.at[i], came.at[2 * i]),
            pltpu.make_async_copy(got.at[:, c, x], held.at[i], came.at[2 * i + 1]),
        ]
        for read in pair:
            read.start()
        reads.append(pair)
    writes = []
    for i, (c, x) in enumerate(parts):
        for read in reads[i]:
            read.wait()
        for m in range(n):
            at = pl.ds(m * rows, rows)
            for k in range(2):
                for j in range(2):
                    num, den = (held[i, m, k, j, v].astype(jnp.float32) for v in range(2))
                    done = merged_of(num, den, prior[i, k, j, at, :])
                    result[i, k, j, at, :] = done.astype(out.dtype)
        writes.append(pltpu.make_async_copy(result.at[i], out.at[c, x, :, high], sent.at[i]))
        writes[-1].start()
    for write in writes:
        write.wait()


def merge_high(got, base, whole, passed):
    n, cores, _, _, _, rows, cols = got.shape
    parts = cores * n // 2
    block = (parts, 2, 2, TILE - LOW, cols)
    return pl.pallas_call(
        merge_high_body,
        out_shape=jax.ShapeDtypeStruct(whole.shape, whole.dtype),
        in_specs=[HBM, HBM, HBM, SMEM],
        out_specs=HBM,
        scratch_shapes=[
            pltpu.VMEM((parts, n, 2, 2, 2, rows, cols), got.dtype),
            pltpu.VMEM(block, base.dtype),
            pltpu.VMEM(block, whole.dtype),
            pltpu.SemaphoreType.DMA((2 * parts,)),
            pltpu.SemaphoreType.DMA((parts,)),
        ],
        input_output_aliases={2: 0},
        name="merge_high",
    )(got, base, whole, passed)


def fence_body(*refs):
    refs[-1][0] = 0


def fence(arrays):
    return pl.pallas_call(
        fence_body,
        out_shape=jax.ShapeDtypeStruct((1,), jnp.int32),
        in_specs=[ANY] * len(arrays),
        out_specs=SMEM,
        compiler_params=PARAMS,
        cost_estimate=LONG,
        name="fence",
    )(*arrays)


def shifted(x, axis, by):
    n = lax.axis_size(axis)
    return lax.ppermute(x, axis, [(i, (i + by) % n) for i in range(n)])


def all_shifted(pieces, axis):
    n = lax.axis_size(axis)
    moved = {d: shifted(pieces[d], axis, d) for d in (*range(1, n, 2), *range(2, n, 2))}
    return [moved[d] for d in range(1, n)]


def over_z(x):
    nz, ny, nx = (lax.axis_size(a) for a in ("z", "task", "shard"))
    groups = [
        [(((j + y) % nz * 2 + c) * ny + y) * nx + x for j in range(nz) for c in range(2)]
        for y in range(ny)
        for x in range(nx)
    ]
    flat = x.reshape(2 * nz, *x.shape[2:])
    return lax.all_to_all(flat, MESH, 0, 0, axis_index_groups=groups, tiled=True).reshape(x.shape)


def local(weights, fisher, base_weights, tile_list, tile_count):
    weights, fisher = weights[0], fisher[0]
    nz, nx, ny = (lax.axis_size(a) for a in ("z", "shard", "task"))
    x = lax.axis_index("shard")
    cols = base_weights.shape[2]
    hold = lax.optimization_barrier

    tiles, counts = tile_list[0, :, :, 0], tile_count[0]
    rows = (TILE - LOW) // ny
    args = (tiles, counts, weights, fisher, nz)
    low, high_2, token = pack(*args, True, rows, (2,), ())
    high_1, high_3, high_0, _ = pack(*args, False, rows, (1, 3, 0), (token,))
    high = [high_0, high_1, high_2, high_3]

    got_low = over_z(low)
    got_high = [high[0]] + all_shifted(high, "task")
    base = base_weights.reshape(2, nx, 2, TILE, cols)
    base, packed = hold((base, high[1]))
    prior = []
    for d in range(nx):
        part = lax.dynamic_index_in_dim(base[:, :, :, :LOW], lax.rem(x + d, nx), 1, keepdims=False)
        prior.append(shifted(part, "shard", d) if d else part)
    far, got_high, prior = hold((got_low[2], got_high, prior))
    far = shifted(far, "task", 2)
    added = add_high(got_high)
    near, added = hold((got_low, added))
    others = [shifted(near[1], "task", 1), far, shifted(near[3], "task", 3)]
    moved = lax.all_to_all(
        added.reshape(-1, *added.shape[2:]), ("z", "core", "shard"), 0, 0, tiled=True
    )
    moved, passed = hold((moved, fence(others[1:2])))
    moved = lax.all_to_all(
        moved.reshape(nz, 2, nx, *moved.shape[1:]), "task", 0, 0, tiled=True
    )

    merged = merge_low(got_low, others, prior, passed)
    whole = place([merged[0]] + all_shifted(merged, "shard"))
    whole = merge_high(moved, base_weights.reshape(whole.shape), whole, passed)
    return whole.reshape(base_weights.shape)


def solution(mesh):
    split = Mesh(
        mesh.devices.reshape(mesh.devices.shape[0] // 2, 2, *mesh.devices.shape[1:]), MESH
    )
    rows = ("z", "core")
    in_specs = (
        P("task", None, ("z", "core", "shard"), None),
        P("task", None, ("z", "core", "shard"), None),
        P(rows, "task", "shard"),
        P("task", None, None, None),
        P("task", None, None),
    )
    return jax.shard_map(
        local, mesh=split, in_specs=in_specs, out_specs=P(rows, "task", "shard"), check_vma=False
    )
```

```python
import functools

import jax
import jax.numpy as jnp
from jax import lax
from jax.experimental import pallas as pl
from jax.experimental.pallas import tpu as pltpu
from jax.sharding import Mesh, PartitionSpec as P

TILE = 128
PRIOR_WEIGHT = 0.5
LOW = 64
LONG = pl.CostEstimate(flops=100_000_000_000, bytes_accessed=0, transcendentals=0)
SHORT = pl.CostEstimate(flops=0, bytes_accessed=0, transcendentals=0)
GRANT = 16 << 20
MESH = ("z", "core", "task", "shard")
ANY = pl.BlockSpec(memory_space=pl.ANY)
HBM = pl.BlockSpec(memory_space=pltpu.HBM)
VMEM = pl.BlockSpec(memory_space=pltpu.VMEM)
SMEM = pl.BlockSpec(memory_space=pltpu.SMEM)
PARAMS = pltpu.CompilerParams(vmem_limit_bytes=GRANT)


def my_block():
    z, c, x = lax.axis_index("z"), lax.axis_index("core"), lax.axis_index("shard")
    return (z * 2 + c) * lax.axis_size("shard") + x


def listed(tiles, counts, e):
    tile = jnp.minimum(jnp.maximum(tiles[e, my_block()], 0), 1)
    sign = jnp.where(counts[e, my_block()] > 0, jnp.where(tile == 0, 1.0, -1.0), 0.0)
    return tile * TILE, sign.astype(jnp.bfloat16)


def pack_body(low, rows, shifts, after, tiles, counts, weights, fisher, *refs):
    refs = refs[after:]
    count = int(low) + len(shifts)
    outs, token, helds, (came, sent) = refs[:count], refs[count], refs[count + 1 : -2], refs[-2:]
    token[0] = 0
    n = helds[0].shape[0]
    y = lax.axis_index("task")
    reads = []
    for j in range(n):
        first = lax.rem(y + j, n) * 2
        for ec in range(2):
            row, sign = listed(tiles, counts, first + ec)
            for k, held in enumerate(helds):
                at = row
                if not low or k:
                    at = at + LOW
                    if len(shifts) == 1:
                        at = at + lax.rem(y + shifts[0], n) * rows
                at = pl.ds(pl.multiple_of(at, 8), held.shape[3])
                for a, src in enumerate((weights, fisher)):
                    read = pltpu.make_async_copy(
                        src.at[first + ec, at], held.at[j, ec, a], came.at[len(reads)]
                    )
                    reads.append((read, held.at[j, ec, a], sign if a else None))
                    read.start()
    writes, per = [], len(reads) // n
    for j in range(n):
        first = lax.rem(y + j, n) * 2
        for read, held, sign in reads[j * per : (j + 1) * per]:
            read.wait()
            if sign is not None:
                held[...] = held[...] * sign
        parts = [(helds[0].at[j], outs[0].at[j])] if low else []
        for d, out in zip(shifts, outs[int(low) :]):
            row = pl.multiple_of(lax.rem(y + d, n) * rows, 8) if len(shifts) > 1 else 0
            parts.append((helds[-1].at[j, :, :, pl.ds(row, rows)], out.at[pl.ds(first, 2)]))
        for src, dst in parts:
            write = pltpu.make_async_copy(src, dst, sent.at[len(writes)])
            writes.append(write)
            write.start()
    for write in writes:
        write.wait()


def pack(tiles, counts, weights, fisher, n, low, rows, shifts, after):
    experts, _, cols = weights.shape
    reads = ([LOW] if low else []) + [n * rows if len(shifts) > 1 else rows]
    shapes = [(n, 2, 2, LOW, cols)] if low else []
    shapes += [(experts, 2, rows, cols)] * len(shifts)
    return pl.pallas_call(
        functools.partial(pack_body, low, rows, shifts, len(after)),
        out_shape=[jax.ShapeDtypeStruct(shape, weights.dtype) for shape in shapes]
        + [jax.ShapeDtypeStruct((1,), jnp.int32)],
        in_specs=[SMEM, SMEM, HBM, HBM] + [SMEM] * len(after),
        out_specs=[HBM] * len(shapes) + [SMEM],
        scratch_shapes=[pltpu.VMEM((n, 2, 2, r, cols), weights.dtype) for r in reads]
        + [
            pltpu.SemaphoreType.DMA((2 * experts * len(reads),)),
            pltpu.SemaphoreType.DMA((n * len(shapes),)),
        ],
        name="pack",
    )(tiles, counts, weights, fisher, *after)


def sums(loads):
    num, den = [0.0, 0.0], [0.0, 0.0]
    for load in loads:
        w, f = (v.astype(jnp.float32) for v in load())
        term = (f * w).astype(jnp.bfloat16).astype(jnp.float32)
        term_0, share_0 = jnp.where(f > 0.0, term, 0.0), jnp.maximum(f, 0.0)
        num = [num[0] + term_0, num[1] + (term_0 - term)]
        den = [den[0] + share_0, den[1] + (share_0 - f)]
    return num, den


def merged_of(num, den, prior):
    return (num + PRIOR_WEIGHT * prior.astype(jnp.float32)) / (den + PRIOR_WEIGHT)


def merge_low_body(n, passed, first, *rest):
    got, base, outs = (first, *rest[: n - 1]), rest[n - 1 : 2 * n - 1], rest[2 * n - 1 :]
    rows, cols = outs[0].shape[2:]
    x = lax.axis_index("shard")
    step = 16
    for d, out in enumerate(outs):
        at = pl.ds(pl.multiple_of(lax.rem(x + d, n) * cols, cols), cols)
        for r in range(0, rows, step):
            loads = [
                lambda g=g: (g[0, 0, pl.ds(r, step), at], g[0, 1, pl.ds(r, step), at]) for g in got
            ]
            num, den = sums(loads)
            for j in range(2):
                prior = base[(n - d) % n][0, j, pl.ds(r, step), :]
                out[0, j, pl.ds(r, step), :] = merged_of(num[j], den[j], prior).astype(out.dtype)


def merge_low(first, others, base, passed):
    n = len(base)
    _, _, _, rows, cols = first.shape
    piece = base[0].shape[3]
    out = jax.ShapeDtypeStruct((2, 2, rows, piece), first.dtype)
    return pl.pallas_call(
        functools.partial(merge_low_body, n),
        out_shape=[out] * n,
        grid=(2,),
        in_specs=[SMEM, pl.BlockSpec((None, 1, 2, rows, cols), lambda i: (0, i, 0, 0, 0))]
        + [pl.BlockSpec((1, 2, rows, cols), lambda i: (i, 0, 0, 0))] * (n - 1)
        + [pl.BlockSpec((1, 2, rows, piece), lambda i: (i, 0, 0, 0))] * n,
        out_specs=[pl.BlockSpec((1, 2, rows, piece), lambda i: (i, 0, 0, 0))] * n,
        compiler_params=PARAMS,
        cost_estimate=LONG,
        name="merge_low",
    )(passed, first, *others, *base)


def add_high_body(n, *refs):
    got, out = refs[:n], refs[n]
    cols = out.shape[-1]
    for e in range(out.shape[0]):
        for x in range(n):
            at = pl.ds(x * cols, cols)
            num, den = sums([lambda g=g: (g[e, 0, :, at], g[e, 1, :, at]) for g in got])
            for j in range(2):
                out[e, x, j, 0] = num[j].astype(out.dtype)
                out[e, x, j, 1] = den[j].astype(out.dtype)


def add_high(got):
    n = len(got)
    experts, _, rows, cols = got[0].shape
    step = 4
    return pl.pallas_call(
        functools.partial(add_high_body, n),
        out_shape=jax.ShapeDtypeStruct((experts, n, 2, 2, rows, cols // n), got[0].dtype),
        grid=(experts // step,),
        in_specs=[pl.BlockSpec((step, 2, rows, cols), lambda i: (i, 0, 0, 0))] * n,
        out_specs=pl.BlockSpec((step, n, 2, 2, rows, cols // n), lambda i: (i, 0, 0, 0, 0, 0)),
        compiler_params=PARAMS,
        cost_estimate=SHORT,
        name="add_high",
    )(*got)


def place_body(n, *refs):
    pieces, out, sem = refs[:n], refs[-2], refs[-1]
    x = lax.axis_index("shard")
    copies = []
    for d, piece in enumerate(pieces):
        came = lax.rem(x + n - d, n)
        for c in range(2):
            copies.append(
                pltpu.make_async_copy(
                    piece.at[c], out.at[c, came, :, pl.ds(0, piece.shape[2])], sem.at[len(copies)]
                )
            )
    for c in copies:
        c.start()
    for c in copies:
        c.wait()


def place(pieces):
    n = len(pieces)
    return pl.pallas_call(
        functools.partial(place_body, n),
        out_shape=jax.ShapeDtypeStruct((2, n, 2, TILE, pieces[0].shape[3]), pieces[0].dtype),
        in_specs=[VMEM] * n,
        out_specs=HBM,
        scratch_shapes=[pltpu.SemaphoreType.DMA((2 * n,))],
        compiler_params=PARAMS,
        cost_estimate=SHORT,
        name="place",
    )(*pieces)


def merge_high_body(got, base, *refs):
    out, held, prior, result, came, sent = refs[-6:]
    n, cores, _, _, _, rows, _ = got.shape
    high = pl.ds(LOW, TILE - LOW)
    parts = [(c, pl.ds(x, 2)) for c in range(cores) for x in range(0, n, 2)]
    reads = []
    for i, (c, x) in enumerate(parts):
        pair = [
            pltpu.make_async_copy(base.at[c, x, :, high], prior.at[i], came.at[2 * i]),
            pltpu.make_async_copy(got.at[:, c, x], held.at[i], came.at[2 * i + 1]),
        ]
        for read in pair:
            read.start()
        reads.append(pair)
    writes = []
    for i, (c, x) in enumerate(parts):
        for read in reads[i]:
            read.wait()
        for m in range(n):
            at = pl.ds(m * rows, rows)
            for k in range(2):
                for j in range(2):
                    num, den = (held[i, m, k, j, v].astype(jnp.float32) for v in range(2))
                    done = merged_of(num, den, prior[i, k, j, at, :])
                    result[i, k, j, at, :] = done.astype(out.dtype)
        writes.append(pltpu.make_async_copy(result.at[i], out.at[c, x, :, high], sent.at[i]))
        writes[-1].start()
    for write in writes:
        write.wait()


def merge_high(got, base, whole, passed):
    n, cores, _, _, _, rows, cols = got.shape
    parts = cores * n // 2
    block = (parts, 2, 2, TILE - LOW, cols)
    return pl.pallas_call(
        merge_high_body,
        out_shape=jax.ShapeDtypeStruct(whole.shape, whole.dtype),
        in_specs=[HBM, HBM, HBM, SMEM],
        out_specs=HBM,
        scratch_shapes=[
            pltpu.VMEM((parts, n, 2, 2, 2, rows, cols), got.dtype),
            pltpu.VMEM(block, base.dtype),
            pltpu.VMEM(block, whole.dtype),
            pltpu.SemaphoreType.DMA((2 * parts,)),
            pltpu.SemaphoreType.DMA((parts,)),
        ],
        input_output_aliases={2: 0},
        name="merge_high",
    )(got, base, whole, passed)


def cut_body(which, whole, out, sem):
    copy = pltpu.make_async_copy(whole.at[which], out, sem)
    copy.start()
    copy.wait()


def cut(whole, which):
    return pl.pallas_call(
        functools.partial(cut_body, which),
        out_shape=jax.ShapeDtypeStruct(whole.shape[1:], whole.dtype),
        in_specs=[HBM],
        out_specs=VMEM,
        scratch_shapes=[pltpu.SemaphoreType.DMA],
        compiler_params=PARAMS,
        cost_estimate=SHORT,
        name="cut",
    )(whole)


def fence_body(*refs):
    refs[-1][0] = 0


def fence(arrays):
    return pl.pallas_call(
        fence_body,
        out_shape=jax.ShapeDtypeStruct((1,), jnp.int32),
        in_specs=[ANY] * len(arrays),
        out_specs=SMEM,
        compiler_params=PARAMS,
        cost_estimate=LONG,
        name="fence",
    )(*arrays)


def shifted(x, axis, by):
    n = lax.axis_size(axis)
    return lax.ppermute(x, axis, [(i, (i + by) % n) for i in range(n)])


def all_shifted(pieces, axis):
    n = lax.axis_size(axis)
    moved = {d: shifted(pieces[d], axis, d) for d in (*range(1, n, 2), *range(2, n, 2))}
    return [moved[d] for d in range(1, n)]


def over_z(x):
    nz, ny, nx = (lax.axis_size(a) for a in ("z", "task", "shard"))
    groups = [
        [(((j + y) % nz * 2 + c) * ny + y) * nx + x for j in range(nz) for c in range(2)]
        for y in range(ny)
        for x in range(nx)
    ]
    flat = x.reshape(2 * nz, *x.shape[2:])
    return lax.all_to_all(flat, MESH, 0, 0, axis_index_groups=groups, tiled=True).reshape(x.shape)


def local(weights, fisher, base_weights, tile_list, tile_count):
    weights, fisher = weights[0], fisher[0]
    nz, nx, ny = (lax.axis_size(a) for a in ("z", "shard", "task"))
    x = lax.axis_index("shard")
    cols = base_weights.shape[2]
    hold = lax.optimization_barrier

    tiles, counts = tile_list[0, :, :, 0], tile_count[0]
    rows = (TILE - LOW) // ny
    args = (tiles, counts, weights, fisher, nz)
    low, high_2, token = pack(*args, True, rows, (2,), ())
    high_1, high_3, high_0, _ = pack(*args, False, rows, (1, 3, 0), (token,))
    high = [high_0, high_1, high_2, high_3]

    got_low = over_z(low)
    got_high = [high[0]] + all_shifted(high, "task")
    base = base_weights.reshape(2, nx, 2, TILE, cols)
    base, packed = hold((base, high[1]))
    prior = []
    for d in range(nx):
        part = lax.dynamic_index_in_dim(base[:, :, :, :LOW], lax.rem(x + d, nx), 1, keepdims=False)
        prior.append(shifted(part, "shard", d) if d else part)
    far, got_high, prior = hold((cut(got_low, 2), got_high, prior))
    far = shifted(far, "task", 2)
    added = add_high(got_high)
    near, added = hold((got_low, added))
    others = [shifted(near[1], "task", 1), far, shifted(near[3], "task", 3)]
    moved = lax.all_to_all(
        added.reshape(-1, *added.shape[2:]), ("z", "core", "shard"), 0, 0, tiled=True
    )
    moved, passed = hold((moved, fence(others[1:2])))
    moved = lax.all_to_all(
        moved.reshape(nz, 2, nx, *moved.shape[1:]), "task", 0, 0, tiled=True
    )

    merged = merge_low(got_low, others, prior, passed)
    whole = place([merged[0]] + all_shifted(merged, "shard"))
    whole = merge_high(moved, base_weights.reshape(whole.shape), whole, passed)
    return whole.reshape(base_weights.shape)


def solution(mesh):
    split = Mesh(
        mesh.devices.reshape(mesh.devices.shape[0] // 2, 2, *mesh.devices.shape[1:]), MESH
    )
    rows = ("z", "core")
    in_specs = (
        P("task", None, ("z", "core", "shard"), None),
        P("task", None, ("z", "core", "shard"), None),
        P(rows, "task", "shard"),
        P("task", None, None, None),
        P("task", None, None),
    )
    return jax.shard_map(
        local, mesh=split, in_specs=in_specs, out_specs=P(rows, "task", "shard"), check_vma=False
    )
```
